256 devices in a mesh: seg: 8 (over z_hi, core), shard: 16 (over x, y), tok: 2 (over z_lo).
Axes of the slice: x: 4, y: 4, z: 8 (z_hi: 4, z_lo: 2; z = z_hi * 2 + z_lo), core: 2. Of those that a mesh axis runs over, the one named last changes fastest.
Arguments:
- activations: bfloat16 [768, 2560], P('tok', 'shard'), may hold values from -6 to 6
- gate_weight: bfloat16 [2560, 10240], P('shard', 'seg'), may hold values from -0.125 to 0.125
- up_weight: bfloat16 [2560, 10240], P('shard', 'seg'), may hold values from -0.125 to 0.125
- down_weight: bfloat16 [10240, 2560], P('seg', 'shard'), may hold values from -0.0625 to 0.0625
- encoder_weight: bfloat16 [2560, 65536], P(None, ('seg', 'shard')), may hold values from -0.125 to 0.125
- encoder_bias: float32 [65536], P(('seg', 'shard')), may hold values from -0.6 to 0.2
- decoder_weight: bfloat16 [65536, 2560], P(('seg', 'shard')), may hold values from -0.0625 to 0.0625
- decoder_bias: float32 [2560], replicated, may hold values from -1.5 to 1.5
- segment_sizes: int32 [8], replicated, may hold values from 4096 to 8192, as said below
Outputs:
- grad_encoder: float32 [2560, 65536], P('tok', ('seg', 'shard'))
- grad_decoder: float32 [65536, 2560], P(('seg', 'shard'), 'tok')
- prefix_mse: float32 [8], P('seg')
The draws below stay inside these ranges and needn't reach their ends.
Inputs may be any that keep to these rules, and one draw needn't show every extreme that they name: `segment_sizes`: at least one segment has all 8192 latents live.
All inputs are finite; a program needn't handle non-finite values.
Results may differ from the reference program's by a relative error of at most 0.0078.
Values may be sent and summed in bfloat16 or wider, within the bound.
No kernel may reach another device: no remote copies, remote signals or barrier semaphores. Data moves between devices by JAX's collectives and lax.ppermute only.
A program may use at most 64 MiB of HBM per device.

```python
import math
import jax
import jax.numpy as jnp

D = 2560
FF = 10240
NSEG = 8
SEG_LAT = 8192
LATENTS = 65536
TOKENS = 768


def draw_segment_sizes(key, part):
    base = jax.random.fold_in(key, 11)
    size_key, pick_key = jax.random.split(base)
    sizes = jax.random.randint(size_key, (NSEG,), SEG_LAT // 2, SEG_LAT + 1)
    full_at = jax.random.randint(pick_key, (), 0, NSEG)
    return jnp.where(jnp.arange(NSEG) == full_at, SEG_LAT, sizes).astype(jnp.int32)


def shard_levels(stream_key, extent, cuts, least, top_value):
    gain = 1.0
    for axis_at, parts in cuts:
        draws = jax.random.uniform(jax.random.fold_in(jax.random.fold_in(stream_key, 6), axis_at), (parts,), jnp.float32, least / len(cuts), top_value / len(cuts))
        gain = gain * jnp.repeat(jnp.exp(draws), extent[axis_at] // parts).reshape((-1,) + (1,) * (len(extent) - 1 - axis_at))
    return gain


def noise(stream_key, dims, scale, reach, cuts=(), kind=jnp.bfloat16):
    level = shard_levels(stream_key, dims, cuts, -0.22, 0.18) if cuts else 1.0
    entries = jax.random.normal(stream_key, dims, jnp.float32) * scale * level
    return jnp.minimum(jnp.maximum(entries, -reach), reach).astype(kind)


def setup_inputs(seed: int = 0) -> dict:
    keys = jax.random.split(jax.random.key(seed), 10)
    activations = noise(keys[0], (TOKENS, D), 1.0, 6.0, ((0, 2), (1, 16)))
    gate_weight = noise(keys[1], (D, FF), D ** -0.5, 0.125, ((0, 16), (1, 8)))
    up_weight = noise(keys[2], (D, FF), D ** -0.5, 0.125, ((0, 16), (1, 8)))
    down_weight = noise(keys[3], (FF, D), FF ** -0.5, 0.0625, ((0, 8), (1, 16)))
    encoder_weight = noise(keys[4], (D, LATENTS), D ** -0.5, 0.125, ((1, 128),))
    encoder_bias = jnp.clip(-0.6 + 0.8 * jax.random.uniform(keys[5], (LATENTS,), jnp.float32) ** shard_levels(keys[5], (LATENTS,), ((0, 128),), -0.2, 0.2), -0.6, 0.2)
    decoder_weight = noise(keys[6], (LATENTS, D), SEG_LAT ** -0.5, 0.0625, ((0, 128),))
    decoder_bias = noise(keys[7], (D,), 0.3, 1.5, (), jnp.float32)
    segment_sizes = draw_segment_sizes(jax.random.fold_in(keys[9], 71), 0)
    return {"activations": activations, "gate_weight": gate_weight, "up_weight": up_weight, "down_weight": down_weight, "encoder_weight": encoder_weight, "encoder_bias": encoder_bias, "decoder_weight": decoder_weight, "decoder_bias": decoder_bias, "segment_sizes": segment_sizes}


def reference(activations, gate_weight, up_weight, down_weight, encoder_weight, encoder_bias, decoder_weight, decoder_bias, segment_sizes):
    gate = jnp.dot(activations, gate_weight, preferred_element_type=jnp.float32)
    up_proj = jnp.dot(activations, up_weight, preferred_element_type=jnp.float32)
    hidden = (jax.nn.gelu(gate, approximate=True) * up_proj).astype(jnp.bfloat16)
    mlp_out = jnp.dot(hidden, down_weight, preferred_element_type=jnp.float32).astype(jnp.bfloat16)
    mlp_float = mlp_out.astype(jnp.float32)
    centered = (mlp_float - decoder_bias).astype(jnp.bfloat16)
    scale = 1.0 / math.sqrt(TOKENS)
    positions = jnp.arange(SEG_LAT, dtype=jnp.int32)
    running = jnp.zeros(mlp_float.shape, jnp.float32)
    code_list, slope_list, error_list, mse_list = ([], [], [], [])
    for segment in range(NSEG):
        first_latent = segment * SEG_LAT
        pre_act = jnp.dot(centered, encoder_weight[:, first_latent:first_latent + SEG_LAT], preferred_element_type=jnp.float32) + encoder_bias[first_latent:first_latent + SEG_LAT]
        live_mask = positions < segment_sizes[segment]
        codes = jnp.where(live_mask, jax.nn.softplus(10.0 * pre_act) / 10.0, 0.0).astype(jnp.bfloat16)
        slope = jnp.where(live_mask, jax.nn.sigmoid(10.0 * pre_act), 0.0)
        running = running + jnp.dot(codes, decoder_weight[first_latent:first_latent + SEG_LAT], preferred_element_type=jnp.float32)
        errors = decoder_bias + running - mlp_float
        code_list.append(codes)
        slope_list.append(slope)
        error_list.append(errors)
        mse_list.append(jnp.sum(errors * errors) / (TOKENS * D))
    later = jnp.zeros(mlp_float.shape, jnp.float32)
    encoder_parts = [None] * NSEG
    decoder_parts = [None] * NSEG
    for segment in reversed(range(NSEG)):
        first_latent = segment * SEG_LAT
        later = later + error_list[segment]
        back = (later * scale).astype(jnp.bfloat16)
        decoder_parts[segment] = jnp.dot(code_list[segment].T, back, preferred_element_type=jnp.float32)
        code_back = jnp.dot(back, decoder_weight[first_latent:first_latent + SEG_LAT].T, preferred_element_type=jnp.float32)
        code_grad = (code_back * slope_list[segment]).astype(jnp.bfloat16)
        encoder_parts[segment] = jnp.dot(centered.T, code_grad, preferred_element_type=jnp.float32)
    return (jnp.concatenate(encoder_parts, axis=1), jnp.concatenate(decoder_parts, axis=0), jnp.stack(mse_list))
```

```python
import math

import jax
import jax.numpy as jnp
from jax import lax
from jax.sharding import PartitionSpec as P

F32 = jnp.float32
BF16 = jnp.bfloat16


def dot(left, right, left_dim, right_dim):
    return lax.dot_general(
        left, right, (((left_dim,), (right_dim,)), ((), ())), preferred_element_type=F32
    )


def core_swap(value):
    count = lax.axis_size("seg")
    return lax.ppermute(value, "seg", [(i, i ^ 1) for i in range(count)])


def chip_shift(value, step):
    count = lax.axis_size("seg")
    return lax.ppermute(value, "seg", [(i, (i + 2 * step) % count) for i in range(count)])


def shard_shift(value, axis, step):
    pairs = []
    for x in range(4):
        for y in range(4):
            to = ((x + step) % 4, y) if axis == 0 else (x, (y + step) % 4)
            pairs.append((4 * x + y, 4 * to[0] + to[1]))
    return lax.ppermute(value, "shard", pairs)


def tok_swap(value):
    return lax.ppermute(value, "tok", [(0, 1), (1, 0)])


def shard_exchange(pieces):
    return lax.all_to_all(pieces, "shard", 0, 0)


def shard_gather(value):
    count = lax.axis_size("shard")
    return shard_exchange(jnp.broadcast_to(value[None], (count,) + value.shape))


def local(
    activations,
    gate_weight,
    up_weight,
    down_weight,
    encoder_weight,
    encoder_bias,
    decoder_weight,
    decoder_bias,
    segment_sizes,
):
    shard_index = lax.axis_index("shard")
    segment_index = lax.axis_index("seg")
    tok_index = lax.axis_index("tok")
    core = segment_index % 2
    shards = lax.axis_size("shard")
    tokens, width_slice = activations.shape
    tokens_all = tokens * lax.axis_size("tok")
    width = decoder_bias.shape[0]
    half = width // 2
    segment_total = segment_sizes.shape[0]

    gate_part = dot(gate_weight, activations, 0, 1).reshape(shards, -1, tokens)
    up_part = dot(up_weight, activations, 0, 1).reshape(shards, -1, tokens)
    both = jnp.concatenate([gate_part.astype(BF16), up_part.astype(BF16)], axis=1)
    both = jnp.sum(shard_exchange(both).astype(F32), axis=0)
    units = both.shape[0] // 2
    hidden_slice = (jax.nn.gelu(both[:units], approximate=True) * both[units:]).astype(BF16)
    hidden = shard_gather(hidden_slice).reshape(-1, tokens)
    down_part = dot(down_weight, hidden, 0, 0).reshape(2, -1, tokens)
    kept = lax.dynamic_index_in_dim(down_part, core, 0, keepdims=False)
    given = lax.dynamic_index_in_dim(down_part, 1 - core, 0, keepdims=False)
    pair_sum = kept + core_swap(given)
    pair_sent = pair_sum.astype(BF16)
    total = pair_sum
    for step in (1, 2, 3):
        total = total + chip_shift(pair_sent, step).astype(F32)
    mine = shard_gather(total.astype(BF16))
    other = core_swap(mine)
    mlp_full = jnp.where(
        core == 0, jnp.stack([mine, other], axis=1), jnp.stack([other, mine], axis=1)
    ).reshape(width, tokens)
    centered = (mlp_full.astype(F32) - decoder_bias[:, None]).astype(BF16)
    centered_other = tok_swap(lax.dynamic_slice_in_dim(centered, (1 - tok_index) * half, half, 0))

    lat_count = encoder_weight.shape[1]
    size_here = jnp.sum(jnp.where(jnp.arange(segment_total) == segment_index, segment_sizes, 0))
    latent_index = shard_index * lat_count + jnp.arange(lat_count)
    live_mask = (latent_index < size_here)[:, None]
    pre_act = dot(encoder_weight, centered, 0, 0) + encoder_bias[:, None]
    codes = jnp.where(live_mask, jax.nn.softplus(10.0 * pre_act) / 10.0, 0.0).astype(BF16)
    slope = jnp.where(live_mask, jax.nn.sigmoid(10.0 * pre_act), 0.0)
    codes_other = tok_swap(codes)

    part = dot(decoder_weight, codes, 0, 0).astype(BF16).reshape(shards, width_slice, tokens)
    my_part = jnp.sum(shard_exchange(part).astype(F32), axis=0)
    parts = lax.all_gather(my_part.astype(BF16), "seg").astype(F32)
    start = shard_index * width_slice
    target = lax.dynamic_slice_in_dim(mlp_full, start, width_slice, 0).astype(F32)
    bias_slice = lax.dynamic_slice_in_dim(decoder_bias, start, width_slice, 0)[:, None]
    base = bias_slice - target
    places = jnp.arange(segment_total)
    up_to = (places <= segment_index).astype(F32)[:, None, None]
    weight = (segment_total - jnp.maximum(places, segment_index)).astype(F32)[:, None, None]
    errors = base + jnp.sum(parts * up_to, axis=0)
    summed = (segment_total - segment_index).astype(F32) * base + jnp.sum(parts * weight, axis=0)
    back_slice = (summed * (1.0 / math.sqrt(tokens_all))).astype(BF16)

    square = jnp.broadcast_to(jnp.sum(errors * errors), (8, 128))
    for axis in (0, 1):
        moved = [shard_shift(square, axis, step) for step in (1, 2, 3)]
        square = square + moved[0] + moved[1] + moved[2]
    square = square + tok_swap(square)
    prefix_mse = square[0, :1] / (tokens_all * width)

    back = shard_gather(back_slice).reshape(width, tokens)
    back_other = tok_swap(lax.dynamic_slice_in_dim(back, (1 - tok_index) * half, half, 0))
    code_acc = dot(decoder_weight, back, 1, 0)
    code_grad = (code_acc * slope).astype(BF16)
    code_grad_other = tok_swap(code_grad)
    back_mine = lax.dynamic_slice_in_dim(back, tok_index * half, half, 0)
    centered_mine = lax.dynamic_slice_in_dim(centered, tok_index * half, half, 0)
    grad_decoder = dot(codes, back_mine, 1, 1) + dot(codes_other, back_other, 1, 1)
    grad_encoder = dot(centered_mine, code_grad, 1, 1) + dot(
        centered_other, code_grad_other, 1, 1
    )
    return (grad_encoder, grad_decoder, prefix_mse)


def solution(mesh):
    in_specs = (
        P("tok", "shard"),
        P("shard", "seg"),
        P("shard", "seg"),
        P("seg", "shard"),
        P(None, ("seg", "shard")),
        P(("seg", "shard")),
        P(("seg", "shard"), None),
        P(),
        P(),
    )
    out_specs = (P("tok", ("seg", "shard")), P(("seg", "shard"), "tok"), P("seg"))
    return jax.shard_map(local, mesh=mesh, in_specs=in_specs, out_specs=out_specs, check_vma=False)
```

```python
import math

import jax
import jax.numpy as jnp
from jax import lax
from jax.experimental.layout import Layout, with_layout_constraint
from jax.sharding import PartitionSpec as P


F32 = jnp.float32
BF16 = jnp.bfloat16


def dot(left, right, left_dim, right_dim):
    return lax.dot_general(
        left, right, (((left_dim,), (right_dim,)), ((), ())), preferred_element_type=F32
    )


def core_swap(value):
    count = lax.axis_size("seg")
    return lax.ppermute(value, "seg", [(i, i ^ 1) for i in range(count)])


def chip_shift(value, step):
    count = lax.axis_size("seg")
    return lax.ppermute(value, "seg", [(i, (i + 2 * step) % count) for i in range(count)])


def tok_swap(value):
    return lax.ppermute(value, "tok", [(0, 1), (1, 0)])


def shard_exchange(pieces):
    return lax.all_to_all(pieces, "shard", 0, 0)


def shard_sum(pieces):
    return jnp.sum(shard_exchange(pieces).astype(F32), axis=0)


def shard_gather(value):
    count = lax.axis_size("shard")
    return shard_exchange(jnp.broadcast_to(value[None], (count,) + value.shape))


def step(
    activations,
    gate_weight,
    up_weight,
    down_weight,
    encoder_weight,
    encoder_bias,
    decoder_weight,
    decoder_bias,
    segment_sizes,
):
    shard_index = lax.axis_index("shard")
    segment_index = lax.axis_index("seg")
    tok_index = lax.axis_index("tok")
    core = segment_index % 2
    shards = lax.axis_size("shard")
    tokens, width_slice = activations.shape
    tokens_all = tokens * lax.axis_size("tok")
    width = decoder_bias.shape[0]
    half = width // 2
    segment_total = segment_sizes.shape[0]

    gate_part = dot(gate_weight, activations, 0, 1).reshape(shards, -1, tokens)
    up_part = dot(up_weight, activations, 0, 1).reshape(shards, -1, tokens)
    both = shard_sum(jnp.concatenate([gate_part.astype(BF16), up_part.astype(BF16)], axis=1))
    units = both.shape[0] // 2
    gate, up = both[:units], both[units:]
    hidden_slice = (jax.nn.gelu(gate, approximate=True) * up).astype(BF16)
    hidden = shard_gather(hidden_slice).reshape(-1, tokens)
    down_part = dot(down_weight, hidden, 0, 0).reshape(2, -1, tokens)
    kept = lax.dynamic_index_in_dim(down_part, core, 0, keepdims=False)
    given = lax.dynamic_index_in_dim(down_part, 1 - core, 0, keepdims=False)
    pair_sum = kept + core_swap(given)
    pair_sent = pair_sum.astype(BF16)
    total = pair_sum
    for step in (1, 2, 3):
        total = total + chip_shift(pair_sent, step).astype(F32)
    mine = shard_gather(total.astype(BF16))
    other = core_swap(mine)
    rows = mine.shape[1]

    def by_core(here, there, dim):
        return jnp.where(
            core == 0,
            jnp.concatenate([here, there], axis=dim),
            jnp.concatenate([there, here], axis=dim),
        )

    def half_of(values, which):
        values = values.reshape((shards, 2, rows) + values.shape[1:])
        return lax.dynamic_index_in_dim(values, which, 1, keepdims=False)

    bias_column = decoder_bias[:, None]
    centered_mine = (mine.astype(F32) - half_of(bias_column, core)).astype(BF16)
    centered_other = (other.astype(F32) - half_of(bias_column, 1 - core)).astype(BF16)
    encoder_mine = half_of(encoder_weight, core).reshape(shards * rows, -1)
    encoder_other = half_of(encoder_weight, 1 - core).reshape(shards * rows, -1)

    def tok_half(pieces, which):
        return lax.dynamic_slice_in_dim(pieces, which * (shards // 2), shards // 2, 0)

    target = by_core(
        lax.dynamic_index_in_dim(mine, shard_index, 0, keepdims=False),
        lax.dynamic_index_in_dim(other, shard_index, 0, keepdims=False),
        0,
    ).astype(F32)
    sent = [tok_half(c, 1 - tok_index) for c in (centered_mine, centered_other)]
    centered_peer = tok_swap(jnp.concatenate(sent, axis=0))

    lat_count = encoder_weight.shape[1]
    size_here = jnp.sum(jnp.where(jnp.arange(segment_total) == segment_index, segment_sizes, 0))
    latent_index = shard_index * lat_count + jnp.arange(lat_count)
    live_mask = (latent_index < size_here)[:, None]
    pre_act = dot(encoder_mine, centered_mine.reshape(-1, tokens), 0, 0)
    pre_act = pre_act + dot(encoder_other, centered_other.reshape(-1, tokens), 0, 0)
    pre_act = pre_act + encoder_bias[:, None]
    codes = jnp.where(live_mask, jax.nn.softplus(10.0 * pre_act) / 10.0, 0.0).astype(BF16)
    slope = jnp.where(live_mask, jax.nn.sigmoid(10.0 * pre_act), 0.0)
    codes_other = tok_swap(codes)

    part = dot(decoder_weight, codes, 0, 0).astype(BF16)
    split = 96
    part = with_layout_constraint(part, Layout((0, 1))).reshape(shards, width_slice, tokens)
    start = shard_index * width_slice
    bias_slice = lax.dynamic_slice_in_dim(decoder_bias, start, width_slice, 0)[:, None]
    base = bias_slice - target
    places = jnp.arange(segment_total)
    up_to = (places <= segment_index).astype(F32)[:, None, None]
    weight = (segment_total - jnp.maximum(places, segment_index)).astype(F32)[:, None, None]
    base_weight = (segment_total - segment_index).astype(F32)
    scale = 1.0 / math.sqrt(tokens_all)

    def seg_step(mine, base):
        parts = lax.all_gather(mine, "seg").astype(F32)
        errors = base + jnp.sum(parts * up_to, axis=0)
        summed = base_weight * base + jnp.sum(parts * weight, axis=0)
        return (summed * scale).astype(BF16), jnp.sum(errors * errors, axis=0, keepdims=True)

    sum_first = shard_sum(part[:, :split]).astype(BF16)
    sum_second = shard_sum(part[:, split:]).astype(BF16)
    slice_first, square_first = seg_step(sum_first, base[:split])
    slice_first, square_first, sum_second = lax.optimization_barrier(
        (slice_first, square_first, sum_second)
    )
    back_first = shard_gather(slice_first)
    slice_second, square_second = seg_step(sum_second, base[split:])

    square = square_first + square_second
    high = square.astype(BF16)
    low = (square - high.astype(F32)).astype(BF16)
    row = lax.broadcasted_iota(jnp.int32, (8, tokens), 0)
    extra = jnp.where(row == 0, high, jnp.where(row == 1, low, jnp.zeros_like(low)))
    back_second = shard_gather(jnp.concatenate([slice_second, extra], axis=0))

    def joined(first, second):
        return jnp.concatenate([first, second], axis=1).reshape(-1, tokens)

    first_other = tok_swap(tok_half(back_first, 1 - tok_index))
    rest = width_slice - split
    second_other = tok_swap(
        lax.dynamic_slice(
            back_second,
            ((1 - tok_index) * (shards // 2), 0, 0),
            (shards // 2, rest, tokens),
        )
    )
    back = joined(back_first, back_second[:, :rest])
    code_acc = dot(decoder_weight, back, 1, 0)
    code_grad = (code_acc * slope).astype(BF16)
    code_grad_other = tok_swap(code_grad)

    squares = jnp.broadcast_to(jnp.sum(back_second[:, rest:].astype(F32)), (8, 128))
    squares = squares + tok_swap(squares)
    prefix_mse = squares[0, :1] / (tokens_all * width)

    back_mine = lax.dynamic_slice_in_dim(back, tok_index * half, half, 0)
    back_other = joined(first_other, second_other)
    grad_decoder = dot(codes, back_mine, 1, 1)
    grad_decoder = grad_decoder + dot(codes_other, back_other, 1, 1)
    count = shards // 2
    own = by_core(tok_half(centered_mine, tok_index), tok_half(centered_other, tok_index), 1)
    own = lax.optimization_barrier(own.reshape(half, tokens))
    peer = by_core(centered_peer[:count], centered_peer[count:], 1)
    peer = lax.optimization_barrier(peer.reshape(half, tokens))
    grad_encoder = dot(own, code_grad, 1, 1)
    grad_encoder = grad_encoder + dot(peer, code_grad_other, 1, 1)
    return (grad_encoder, grad_decoder, prefix_mse)


def solution(mesh):
    in_specs = (
        P("tok", "shard"),
        P("shard", "seg"),
        P("shard", "seg"),
        P("seg", "shard"),
        P(None, ("seg", "shard")),
        P(("seg", "shard")),
        P(("seg", "shard"), None),
        P(),
        P(),
    )
    out_specs = (P("tok", ("seg", "shard")), P(("seg", "shard"), "tok"), P("seg"))
    return jax.shard_map(step, mesh=mesh, in_specs=in_specs, out_specs=out_specs, check_vma=False)
```

```python
import math

import jax
import jax.numpy as jnp
from jax import lax
from jax.experimental.layout import Layout, with_layout_constraint
from jax.sharding import PartitionSpec as P


F32 = jnp.float32
BF16 = jnp.bfloat16


def dot(left, right, left_dim, right_dim):
    return lax.dot_general(
        left, right, (((left_dim,), (right_dim,)), ((), ())), preferred_element_type=F32
    )


def core_swap(value):
    count = lax.axis_size("seg")
    return lax.ppermute(value, "seg", [(i, i ^ 1) for i in range(count)])


def chip_shift(value, step):
    count = lax.axis_size("seg")
    return lax.ppermute(value, "seg", [(i, (i + 2 * step) % count) for i in range(count)])


def tok_swap(value):
    return lax.ppermute(value, "tok", [(0, 1), (1, 0)])


def shard_exchange(pieces):
    return lax.all_to_all(pieces, "shard", 0, 0)


def shard_sum(pieces):
    return jnp.sum(shard_exchange(pieces).astype(F32), axis=0)


def shard_gather(value):
    count = lax.axis_size("shard")
    return shard_exchange(jnp.broadcast_to(value[None], (count,) + value.shape))


def step(
    activations,
    gate_weight,
    up_weight,
    down_weight,
    encoder_weight,
    encoder_bias,
    decoder_weight,
    decoder_bias,
    segment_sizes,
):
    shard_index = lax.axis_index("shard")
    segment_index = lax.axis_index("seg")
    tok_index = lax.axis_index("tok")
    core = segment_index % 2
    shards = lax.axis_size("shard")
    tokens, _ = activations.shape
    tokens_all = tokens * lax.axis_size("tok")
    width = decoder_bias.shape[0]
    half = width // 2
    segment_total = segment_sizes.shape[0]

    gate_part = dot(gate_weight, activations, 0, 1).reshape(shards, -1, tokens)
    up_part = dot(up_weight, activations, 0, 1).reshape(shards, -1, tokens)
    both = shard_sum(jnp.concatenate([gate_part.astype(BF16), up_part.astype(BF16)], axis=1))
    units = both.shape[0] // 2
    gate, up = both[:units], both[units:]
    hidden_slice = (jax.nn.gelu(gate, approximate=True) * up).astype(BF16)
    hidden = shard_gather(hidden_slice).reshape(-1, tokens)
    down_part = dot(down_weight, hidden, 0, 0).reshape(2, -1, tokens)
    kept = lax.dynamic_index_in_dim(down_part, core, 0, keepdims=False)
    given = lax.dynamic_index_in_dim(down_part, 1 - core, 0, keepdims=False)
    pair_sum = kept + core_swap(given)
    pair_sent = pair_sum.astype(BF16)
    total = pair_sum
    for step in (1, 2, 3):
        total = total + chip_shift(pair_sent, step).astype(F32)
    mine = shard_gather(total.astype(BF16))
    other = core_swap(mine)
    rows = mine.shape[1]

    def by_core(here, there, dim):
        return jnp.where(
            core == 0,
            jnp.concatenate([here, there], axis=dim),
            jnp.concatenate([there, here], axis=dim),
        )

    def half_of(values, which):
        values = values.reshape((shards, 2, rows) + values.shape[1:])
        return lax.dynamic_index_in_dim(values, which, 1, keepdims=False)

    bias_column = decoder_bias[:, None]
    centered_mine = (mine.astype(F32) - half_of(bias_column, core)).astype(BF16)
    centered_other = (other.astype(F32) - half_of(bias_column, 1 - core)).astype(BF16)
    encoder_mine = half_of(encoder_weight, core).reshape(shards * rows, -1)
    encoder_other = half_of(encoder_weight, 1 - core).reshape(shards * rows, -1)

    def tok_half(pieces, which):
        return lax.dynamic_slice_in_dim(pieces, which * (shards // 2), shards // 2, 0)

    sent = [tok_half(c, 1 - tok_index) for c in (centered_mine, centered_other)]
    centered_peer = tok_swap(jnp.concatenate(sent, axis=0))

    lat_count = encoder_weight.shape[1]
    size_here = jnp.sum(jnp.where(jnp.arange(segment_total) == segment_index, segment_sizes, 0))
    latent_index = shard_index * lat_count + jnp.arange(lat_count)
    live_mask = (latent_index < size_here)[:, None]
    pre_act = dot(encoder_mine, centered_mine.reshape(-1, tokens), 0, 0)
    pre_act = pre_act + dot(encoder_other, centered_other.reshape(-1, tokens), 0, 0)
    pre_act = pre_act + encoder_bias[:, None]
    codes = jnp.where(live_mask, jax.nn.softplus(10.0 * pre_act) / 10.0, 0.0).astype(BF16)
    slope = jnp.where(live_mask, jax.nn.sigmoid(10.0 * pre_act), 0.0)
    codes_other = tok_swap(codes)

    count = shards // 2
    cut = 3 * half // 5
    rows_a, rows_b = cut // count, (half - cut) // count

    def columns_of(low, high):
        return lax.optimization_barrier(
            jnp.concatenate(
                [decoder_weight[:, low:high], decoder_weight[:, half + low : half + high]], axis=1
            )
        )

    decoder_a = columns_of(0, cut)
    decoder_b = columns_of(cut, half)
    mlp_full = lax.optimization_barrier(by_core(mine, other, 1).reshape(width, tokens))
    half_start = (shard_index // count) * half

    def base_of(offset, size):
        start = half_start + offset + (shard_index % count) * size
        bias = lax.dynamic_slice_in_dim(decoder_bias, start, size, 0)[:, None]
        return bias - lax.dynamic_slice_in_dim(mlp_full, start, size, 0).astype(F32)

    base_a, base_b = base_of(0, rows_a), base_of(cut, rows_b)

    def part_of(columns, size):
        part = with_layout_constraint(dot(columns, codes, 0, 0).astype(BF16), Layout((0, 1)))
        return part.reshape(shards, size, tokens)

    places = jnp.arange(segment_total)
    up_to = (places <= segment_index).astype(F32)[:, None, None]
    weight = (segment_total - jnp.maximum(places, segment_index)).astype(F32)[:, None, None]
    base_weight = (segment_total - segment_index).astype(F32)
    scale = 1.0 / math.sqrt(tokens_all)

    def seg_step(mine, base):
        parts = lax.all_gather(mine, "seg").astype(F32)
        errors = base + jnp.sum(parts * up_to, axis=0)
        summed = base_weight * base + jnp.sum(parts * weight, axis=0)
        return (summed * scale).astype(BF16), jnp.sum(errors * errors, axis=0, keepdims=True)

    sum_first = shard_sum(part_of(decoder_a, rows_a)).astype(BF16)
    sum_second = shard_sum(part_of(decoder_b, rows_b)).astype(BF16)
    slice_first, square_first = seg_step(sum_first, base_a)
    slice_first, square_first, sum_second = lax.optimization_barrier(
        (slice_first, square_first, sum_second)
    )
    back_first = shard_gather(slice_first)
    slice_second, square_second = seg_step(sum_second, base_b)

    square = square_first + square_second
    high = square.astype(BF16)
    low = (square - high.astype(F32)).astype(BF16)
    row = lax.broadcasted_iota(jnp.int32, (8, tokens), 0)
    extra = jnp.where(row == 0, high, jnp.where(row == 1, low, jnp.zeros_like(low)))
    back_second = shard_gather(jnp.concatenate([slice_second, extra], axis=0))

    first_other = tok_swap(tok_half(back_first, 1 - tok_index))
    second_other = tok_swap(
        lax.dynamic_slice(
            back_second, ((1 - tok_index) * count, 0, 0), (count, rows_b, tokens)
        )
    )
    acc_first = dot(decoder_a, back_first.reshape(-1, tokens), 1, 0)
    acc_first = lax.optimization_barrier(acc_first)
    acc_second = dot(decoder_b, back_second[:, :rows_b].reshape(-1, tokens), 1, 0)
    code_grad = ((acc_first + acc_second) * slope).astype(BF16)
    code_grad_other = tok_swap(code_grad)

    squares = jnp.broadcast_to(jnp.sum(back_second[:, rows_b:].astype(F32)), (8, 128))
    squares = squares + tok_swap(squares)
    prefix_mse = squares[0, :1] / (tokens_all * width)

    def joined(first, second):
        return jnp.concatenate([first.reshape(-1, tokens), second.reshape(-1, tokens)], axis=0)

    back_mine = joined(
        tok_half(back_first, tok_index),
        lax.dynamic_slice(back_second, (tok_index * count, 0, 0), (count, rows_b, tokens)),
    )
    back_other = joined(first_other, second_other)
    grad_decoder = dot(codes, back_mine, 1, 1)
    grad_decoder = grad_decoder + dot(codes_other, back_other, 1, 1)
    own = by_core(tok_half(centered_mine, tok_index), tok_half(centered_other, tok_index), 1)
    own = lax.optimization_barrier(own.reshape(half, tokens))
    peer = by_core(centered_peer[:count], centered_peer[count:], 1)
    peer = lax.optimization_barrier(peer.reshape(half, tokens))
    grad_encoder = dot(own, code_grad, 1, 1)
    grad_encoder = grad_encoder + dot(peer, code_grad_other, 1, 1)
    return (grad_encoder, grad_decoder, prefix_mse)


def solution(mesh):
    in_specs = (
        P("tok", "shard"),
        P("shard", "seg"),
        P("shard", "seg"),
        P("seg", "shard"),
        P(None, ("seg", "shard")),
        P(("seg", "shard")),
        P(("seg", "shard"), None),
        P(),
        P(),
    )
    out_specs = (P("tok", ("seg", "shard")), P(("seg", "shard"), "tok"), P("seg"))
    return jax.shard_map(step, mesh=mesh, in_specs=in_specs, out_specs=out_specs, check_vma=False)
```

```python
import math

import jax
import jax.numpy as jnp
from jax import lax
from jax.experimental.layout import Layout, with_layout_constraint
from jax.sharding import PartitionSpec as P


F32 = jnp.float32
BF16 = jnp.bfloat16


def dot(left, right, left_dim, right_dim):
    return lax.dot_general(
        left, right, (((left_dim,), (right_dim,)), ((), ())), preferred_element_type=F32
    )


def core_swap(value):
    count = lax.axis_size("seg")
    return lax.ppermute(value, "seg", [(i, i ^ 1) for i in range(count)])


def chip_gather(value):
    count = lax.axis_size("seg")
    groups = [[i for i in range(count) if i % 2 == core] for core in range(2)]
    return lax.all_gather(value, "seg", axis_index_groups=groups)


def tok_swap(value):
    return lax.ppermute(value, "tok", [(0, 1), (1, 0)])


def shard_exchange(pieces):
    return lax.all_to_all(pieces, "shard", 0, 0)


def shard_sum(pieces):
    return jnp.sum(shard_exchange(pieces).astype(F32), axis=0)


def shard_gather(value):
    count = lax.axis_size("shard")
    return shard_exchange(jnp.broadcast_to(value[None], (count,) + value.shape))


def step(
    activations,
    gate_weight,
    up_weight,
    down_weight,
    encoder_weight,
    encoder_bias,
    decoder_weight,
    decoder_bias,
    segment_sizes,
):
    shard_index = lax.axis_index("shard")
    segment_index = lax.axis_index("seg")
    tok_index = lax.axis_index("tok")
    core = segment_index % 2
    shards = lax.axis_size("shard")
    tokens, _ = activations.shape
    tokens_all = tokens * lax.axis_size("tok")
    width = decoder_bias.shape[0]
    half = width // 2
    segment_total = segment_sizes.shape[0]

    gate_part = dot(gate_weight, activations, 0, 1).reshape(shards, -1, tokens)
    up_part = dot(up_weight, activations, 0, 1).reshape(shards, -1, tokens)
    both = shard_sum(jnp.concatenate([gate_part.astype(BF16), up_part.astype(BF16)], axis=1))
    units = both.shape[0] // 2
    gate, up = both[:units], both[units:]
    hidden_slice = (jax.nn.gelu(gate, approximate=True) * up).astype(BF16)
    hidden = shard_gather(hidden_slice).reshape(-1, tokens)
    down_part = dot(down_weight, hidden, 0, 0).reshape(2, -1, tokens)
    kept = lax.dynamic_index_in_dim(down_part, core, 0, keepdims=False)
    given = lax.dynamic_index_in_dim(down_part, 1 - core, 0, keepdims=False)
    pair_sum = kept + core_swap(given)
    pair_sent = pair_sum.astype(BF16)
    total = jnp.sum(chip_gather(pair_sent).astype(F32), axis=0)
    mine = shard_gather(total.astype(BF16))
    other = core_swap(mine)
    rows = mine.shape[1]

    def by_core(here, there, dim):
        return jnp.where(
            core == 0,
            jnp.concatenate([here, there], axis=dim),
            jnp.concatenate([there, here], axis=dim),
        )

    def half_of(values, which):
        values = values.reshape((shards, 2, rows) + values.shape[1:])
        return lax.dynamic_index_in_dim(values, which, 1, keepdims=False)

    bias_column = decoder_bias[:, None]
    centered_mine = (mine.astype(F32) - half_of(bias_column, core)).astype(BF16)
    centered_other = (other.astype(F32) - half_of(bias_column, 1 - core)).astype(BF16)
    encoder_mine = half_of(encoder_weight, core).reshape(shards * rows, -1)
    encoder_other = half_of(encoder_weight, 1 - core).reshape(shards * rows, -1)

    def tok_half(pieces, which):
        return lax.dynamic_slice_in_dim(pieces, which * (shards // 2), shards // 2, 0)

    sent = [tok_half(c, 1 - tok_index) for c in (centered_mine, centered_other)]
    centered_peer = tok_swap(jnp.concatenate(sent, axis=0))

    lat_count = encoder_weight.shape[1]
    size_here = jnp.sum(jnp.where(jnp.arange(segment_total) == segment_index, segment_sizes, 0))
    latent_index = shard_index * lat_count + jnp.arange(lat_count)
    live_mask = (latent_index < size_here)[:, None]
    pre_act = dot(encoder_mine, centered_mine.reshape(-1, tokens), 0, 0)
    pre_act = pre_act + dot(encoder_other, centered_other.reshape(-1, tokens), 0, 0)
    pre_act = pre_act + encoder_bias[:, None]
    codes = jnp.where(live_mask, jax.nn.softplus(10.0 * pre_act) / 10.0, 0.0).astype(BF16)
    slope = jnp.where(live_mask, jax.nn.sigmoid(10.0 * pre_act), 0.0)
    codes_other = tok_swap(codes)

    count = shards // 2
    cut = 3 * half // 5
    rows_a, rows_b = cut // count, (half - cut) // count

    def columns_of(low, high):
        return lax.optimization_barrier(
            jnp.concatenate(
                [decoder_weight[:, low:high], decoder_weight[:, half + low : half + high]], axis=1
            )
        )

    decoder_a = columns_of(0, cut)
    decoder_b = columns_of(cut, half)
    mlp_full = lax.optimization_barrier(by_core(mine, other, 1).reshape(width, tokens))
    half_start = (shard_index // count) * half

    def base_of(offset, size):
        start = half_start + offset + (shard_index % count) * size
        bias = lax.dynamic_slice_in_dim(decoder_bias, start, size, 0)[:, None]
        return bias - lax.dynamic_slice_in_dim(mlp_full, start, size, 0).astype(F32)

    base_a, base_b = base_of(0, rows_a), base_of(cut, rows_b)

    def part_of(columns, size):
        part = with_layout_constraint(dot(columns, codes, 0, 0).astype(BF16), Layout((0, 1)))
        return part.reshape(shards, size, tokens)

    places = jnp.arange(segment_total)
    up_to = (places <= segment_index).astype(F32)[:, None, None]
    weight = (segment_total - jnp.maximum(places, segment_index)).astype(F32)[:, None, None]
    base_weight = (segment_total - segment_index).astype(F32)
    scale = 1.0 / math.sqrt(tokens_all)

    def seg_step(mine, base):
        parts = lax.all_gather(mine, "seg").astype(F32)
        errors = base + jnp.sum(parts * up_to, axis=0)
        summed = base_weight * base + jnp.sum(parts * weight, axis=0)
        return (summed * scale).astype(BF16), jnp.sum(errors * errors, axis=0, keepdims=True)

    sum_first = shard_sum(part_of(decoder_a, rows_a)).astype(BF16)
    sum_second = shard_sum(part_of(decoder_b, rows_b)).astype(BF16)
    slice_first, square_first = seg_step(sum_first, base_a)
    slice_first, square_first, sum_second = lax.optimization_barrier(
        (slice_first, square_first, sum_second)
    )
    back_first = shard_gather(slice_first)
    slice_second, square_second = seg_step(sum_second, base_b)

    square = square_first + square_second
    high = square.astype(BF16)
    low = (square - high.astype(F32)).astype(BF16)
    row = lax.broadcasted_iota(jnp.int32, (8, tokens), 0)
    extra = jnp.where(row == 0, high, jnp.where(row == 1, low, jnp.zeros_like(low)))
    back_second = shard_gather(jnp.concatenate([slice_second, extra], axis=0))

    first_other = tok_swap(tok_half(back_first, 1 - tok_index))
    second_other = tok_swap(
        lax.dynamic_slice(
            back_second, ((1 - tok_index) * count, 0, 0), (count, rows_b, tokens)
        )
    )
    acc_first = dot(decoder_a, back_first.reshape(-1, tokens), 1, 0)
    acc_first = lax.optimization_barrier(acc_first)
    acc_second = dot(decoder_b, back_second[:, :rows_b].reshape(-1, tokens), 1, 0)
    code_grad = ((acc_first + acc_second) * slope).astype(BF16)
    code_grad_other = tok_swap(code_grad)

    squares = jnp.broadcast_to(jnp.sum(back_second[:, rows_b:].astype(F32)), (8, 128))
    squares = squares + tok_swap(squares)
    prefix_mse = squares[0, :1] / (tokens_all * width)

    def joined(first, second):
        return jnp.concatenate([first.reshape(-1, tokens), second.reshape(-1, tokens)], axis=0)

    back_mine = joined(
        tok_half(back_first, tok_index),
        lax.dynamic_slice(back_second, (tok_index * count, 0, 0), (count, rows_b, tokens)),
    )
    back_other = joined(first_other, second_other)
    grad_decoder = dot(codes, back_mine, 1, 1)
    grad_decoder = grad_decoder + dot(codes_other, back_other, 1, 1)
    own = by_core(tok_half(centered_mine, tok_index), tok_half(centered_other, tok_index), 1)
    own = lax.optimization_barrier(own.reshape(half, tokens))
    peer = by_core(centered_peer[:count], centered_peer[count:], 1)
    peer = lax.optimization_barrier(peer.reshape(half, tokens))
    grad_encoder = dot(own, code_grad, 1, 1)
    grad_encoder = grad_encoder + dot(peer, code_grad_other, 1, 1)
    return (grad_encoder, grad_decoder, prefix_mse)


def solution(mesh):
    in_specs = (
        P("tok", "shard"),
        P("shard", "seg"),
        P("shard", "seg"),
        P("seg", "shard"),
        P(None, ("seg", "shard")),
        P(("seg", "shard")),
        P(("seg", "shard"), None),
        P(),
        P(),
    )
    out_specs = (P("tok", ("seg", "shard")), P(("seg", "shard"), "tok"), P("seg"))
    return jax.shard_map(step, mesh=mesh, in_specs=in_specs, out_specs=out_specs, check_vma=False)
```

```python
import math

import jax
import jax.numpy as jnp
from jax import lax
from jax.experimental.layout import Layout, with_layout_constraint
from jax.sharding import PartitionSpec as P


F32 = jnp.float32
BF16 = jnp.bfloat16


def dot(left, right, left_dim, right_dim):
    return lax.dot_general(
        left, right, (((left_dim,), (right_dim,)), ((), ())), preferred_element_type=F32
    )


def core_swap(value):
    count = lax.axis_size("seg")
    return lax.ppermute(value, "seg", [(i, i ^ 1) for i in range(count)])


def chip_shift(value, step):
    count = lax.axis_size("seg")
    return lax.ppermute(value, "seg", [(i, (i + 2 * step) % count) for i in range(count)])


def tok_swap(value):
    return lax.ppermute(value, "tok", [(0, 1), (1, 0)])


def shard_exchange(pieces):
    return lax.all_to_all(pieces, "shard", 0, 0)


def shard_sum(pieces):
    return jnp.sum(shard_exchange(pieces).astype(F32), axis=0)


def shard_gather(value):
    count = lax.axis_size("shard")
    return shard_exchange(jnp.broadcast_to(value[None], (count,) + value.shape))


def step(
    activations,
    gate_weight,
    up_weight,
    down_weight,
    encoder_weight,
    encoder_bias,
    decoder_weight,
    decoder_bias,
    segment_sizes,
):
    shard_index = lax.axis_index("shard")
    segment_index = lax.axis_index("seg")
    tok_index = lax.axis_index("tok")
    core = segment_index % 2
    shards = lax.axis_size("shard")
    tokens, _ = activations.shape
    tokens_all = tokens * lax.axis_size("tok")
    width = decoder_bias.shape[0]
    half = width // 2
    segment_total = segment_sizes.shape[0]

    gate_part = dot(gate_weight, activations, 0, 1).reshape(shards, -1, tokens)
    up_part = dot(up_weight, activations, 0, 1).reshape(shards, -1, tokens)
    both = shard_sum(jnp.concatenate([gate_part.astype(BF16), up_part.astype(BF16)], axis=1))
    units = both.shape[0] // 2
    gate, up = both[:units], both[units:]
    hidden_slice = (jax.nn.gelu(gate, approximate=True) * up).astype(BF16)
    hidden = shard_gather(hidden_slice).reshape(-1, tokens)
    down_part = dot(down_weight, hidden, 0, 0).reshape(2, -1, tokens)
    kept = lax.dynamic_index_in_dim(down_part, core, 0, keepdims=False)
    given = lax.dynamic_index_in_dim(down_part, 1 - core, 0, keepdims=False)
    pair_sum = kept + core_swap(given)
    pair_sent = pair_sum.astype(BF16)
    total = pair_sum
    for step in (1, 2, 3):
        total = total + chip_shift(pair_sent, step).astype(F32)
    mine = shard_gather(total.astype(BF16))
    other = core_swap(mine)
    rows = mine.shape[1]

    def by_core(here, there, dim):
        return jnp.where(
            core == 0,
            jnp.concatenate([here, there], axis=dim),
            jnp.concatenate([there, here], axis=dim),
        )

    def half_of(values, which):
        values = values.reshape((shards, 2, rows) + values.shape[1:])
        return lax.dynamic_index_in_dim(values, which, 1, keepdims=False)

    bias_column = decoder_bias[:, None]
    centered_mine = (mine.astype(F32) - half_of(bias_column, core)).astype(BF16)
    centered_other = (other.astype(F32) - half_of(bias_column, 1 - core)).astype(BF16)
    encoder_mine = half_of(encoder_weight, core).reshape(shards * rows, -1)
    encoder_other = half_of(encoder_weight, 1 - core).reshape(shards * rows, -1)

    def tok_half(pieces, which):
        return lax.dynamic_slice_in_dim(pieces, which * (shards // 2), shards // 2, 0)

    peer_mine = tok_swap(tok_half(centered_mine, 1 - tok_index))
    peer_other = tok_swap(tok_half(centered_other, 1 - tok_index))

    lat_count = encoder_weight.shape[1]
    size_here = jnp.sum(jnp.where(jnp.arange(segment_total) == segment_index, segment_sizes, 0))
    latent_index = shard_index * lat_count + jnp.arange(lat_count)
    live_mask = (latent_index < size_here)[:, None]
    pre_act = dot(encoder_mine, centered_mine.reshape(-1, tokens), 0, 0)
    pre_act = pre_act + dot(encoder_other, centered_other.reshape(-1, tokens), 0, 0)
    pre_act = pre_act + encoder_bias[:, None]
    codes = jnp.where(live_mask, jax.nn.softplus(10.0 * pre_act) / 10.0, 0.0).astype(BF16)
    slope = jnp.where(live_mask, jax.nn.sigmoid(10.0 * pre_act), 0.0)
    codes_other = tok_swap(codes)

    count = shards // 2
    cut = 3 * half // 5
    rows_a, rows_b = cut // count, (half - cut) // count

    def columns_of(low, high):
        return lax.optimization_barrier(
            jnp.concatenate(
                [decoder_weight[:, low:high], decoder_weight[:, half + low : half + high]], axis=1
            )
        )

    decoder_a = columns_of(0, cut)
    decoder_b = columns_of(cut, half)
    mlp_full = lax.optimization_barrier(by_core(mine, other, 1).reshape(width, tokens))
    half_start = (shard_index // count) * half

    def base_of(offset, size):
        start = half_start + offset + (shard_index % count) * size
        bias = lax.dynamic_slice_in_dim(decoder_bias, start, size, 0)[:, None]
        return bias - lax.dynamic_slice_in_dim(mlp_full, start, size, 0).astype(F32)

    base_a, base_b = base_of(0, rows_a), base_of(cut, rows_b)

    def part_of(columns, size):
        part = with_layout_constraint(dot(columns, codes, 0, 0).astype(BF16), Layout((0, 1)))
        return part.reshape(shards, size, tokens)

    places = jnp.arange(segment_total)
    up_to = (places <= segment_index).astype(F32)[:, None, None]
    weight = (segment_total - jnp.maximum(places, segment_index)).astype(F32)[:, None, None]
    base_weight = (segment_total - segment_index).astype(F32)
    scale = 1.0 / math.sqrt(tokens_all)

    def seg_step(mine, base):
        parts = lax.all_gather(mine, "seg").astype(F32)
        errors = base + jnp.sum(parts * up_to, axis=0)
        summed = base_weight * base + jnp.sum(parts * weight, axis=0)
        return (summed * scale).astype(BF16), jnp.sum(errors * errors, axis=0, keepdims=True)

    sum_first = shard_sum(part_of(decoder_a, rows_a)).astype(BF16)
    sum_second = shard_sum(part_of(decoder_b, rows_b)).astype(BF16)
    slice_first, square_first = seg_step(sum_first, base_a)
    slice_first, square_first, sum_second = lax.optimization_barrier(
        (slice_first, square_first, sum_second)
    )
    back_first = shard_gather(slice_first)
    slice_second, square_second = seg_step(sum_second, base_b)

    square = square_first + square_second
    high = square.astype(BF16)
    low = (square - high.astype(F32)).astype(BF16)
    row = lax.broadcasted_iota(jnp.int32, (8, tokens), 0)
    extra = jnp.where(row == 0, high, jnp.where(row == 1, low, jnp.zeros_like(low)))
    back_second = shard_gather(jnp.concatenate([slice_second, extra], axis=0))

    first_other = tok_swap(tok_half(back_first, 1 - tok_index))
    second_other = tok_swap(
        lax.dynamic_slice(
            back_second, ((1 - tok_index) * count, 0, 0), (count, rows_b, tokens)
        )
    )
    acc_first = dot(decoder_a, back_first.reshape(-1, tokens), 1, 0)
    acc_first = lax.optimization_barrier(acc_first)
    acc_second = dot(decoder_b, back_second[:, :rows_b].reshape(-1, tokens), 1, 0)
    code_grad = ((acc_first + acc_second) * slope).astype(BF16)
    code_grad_other = tok_swap(code_grad)

    squares = jnp.broadcast_to(jnp.sum(back_second[:, rows_b:].astype(F32)), (8, 128))
    squares = squares + tok_swap(squares)
    prefix_mse = squares[0, :1] / (tokens_all * width)

    def joined(first, second):
        return jnp.concatenate([first.reshape(-1, tokens), second.reshape(-1, tokens)], axis=0)

    back_mine = joined(
        tok_half(back_first, tok_index),
        lax.dynamic_slice(back_second, (tok_index * count, 0, 0), (count, rows_b, tokens)),
    )
    back_other = joined(first_other, second_other)
    grad_decoder = dot(codes, back_mine, 1, 1)
    grad_decoder = grad_decoder + dot(codes_other, back_other, 1, 1)
    own = by_core(tok_half(centered_mine, tok_index), tok_half(centered_other, tok_index), 1)
    own = lax.optimization_barrier(own.reshape(half, tokens))
    peer = by_core(peer_mine, peer_other, 1)
    peer = lax.optimization_barrier(peer.reshape(half, tokens))
    grad_encoder = dot(own, code_grad, 1, 1)
    grad_encoder = grad_encoder + dot(peer, code_grad_other, 1, 1)
    return (grad_encoder, grad_decoder, prefix_mse)


def solution(mesh):
    in_specs = (
        P("tok", "shard"),
        P("shard", "seg"),
        P("shard", "seg"),
        P("seg", "shard"),
        P(None, ("seg", "shard")),
        P(("seg", "shard")),
        P(("seg", "shard"), None),
        P(),
        P(),
    )
    out_specs = (P("tok", ("seg", "shard")), P(("seg", "shard"), "tok"), P("seg"))
    return jax.shard_map(step, mesh=mesh, in_specs=in_specs, out_specs=out_specs, check_vma=False)
```
